128 devices in a mesh: expert: 4 (over y), blk: 32 (over z, x, core).
Axes of the slice: x: 4, y: 4, z: 4, core: 2. Of those that a mesh axis runs over, the one named last changes fastest.
Arguments:
- tokens: bfloat16 [2, 512, 6144], P(None, 'expert', 'blk'), may hold values from -6 to 6
- expert_ids: int32 [2, 512, 2], P(None, 'expert'), may hold values from 0 to 3, all different within a row; in each aligned block of 128 rows (0 to 127, 128 to 255, ..., all dimensions but the last counted through in order) at most 128 rows name the same one
- route_share: float32 [2, 512], P(None, 'expert'), may hold values from 0.1 to 0.9
- gate_weight: bfloat16 [4, 6144, 16384], P('expert', None, 'blk'), may hold values from -0.078125 to 0.078125
- up_weight: bfloat16 [4, 6144, 16384], P('expert', None, 'blk'), may hold values from -0.078125 to 0.078125
- down_weight: bfloat16 [4, 16384, 6144], P('expert', 'blk'), may hold values from -0.09375 to 0.09375
Outputs:
- combined: bfloat16 [2, 512, 6144], P(None, 'expert', 'blk')
The draws below stay inside these ranges and needn't reach their ends.
Inputs may be any that keep to these rules, and one draw needn't show every extreme that they name: `expert_ids`: each row names two different experts.
All inputs are finite; a program needn't handle non-finite values.
Results may differ from the reference program's by a relative error of at most 0.023.
Values may be sent and summed in bfloat16 or wider, within the bound.
No kernel may reach another device: no remote copies, remote signals or barrier semaphores. Data moves between devices by JAX's collectives and lax.ppermute only.
A program may use at most 128 MiB of HBM per device.

```python
import math
import jax
import jax.numpy as jnp
import numpy as np
from jax import lax

D = 6144
FF = 16384
ROW_DEV = 128
STEPS = 2
EXPERTS = 4
ROWS = 512
N_BLK = 32


def raised(values, key, source, target, blocks, factor):
    owner, partner = [(jnp.arange(values.shape[dim]) // (values.shape[dim] // blocks)).reshape([-1 if axis == dim else 1 for axis in range(values.ndim)]) for dim in (source, target)]
    chosen = jax.random.permutation(key, blocks)[partner]
    strong = (owner == chosen) | (owner == (partner + blocks // 2) % blocks)
    return jnp.where(strong, factor * values, values)


def block_levels(rng, dims, split, smallest, top_value):
    factor_of = 1.0
    for dim, parts in split:
        heights = jax.random.uniform(jax.random.fold_in(jax.random.fold_in(rng, 6), dim), (parts,), jnp.float32, smallest / len(split), top_value / len(split))
        factor_of = factor_of * jnp.repeat(jnp.exp(heights), dims[dim] // parts).reshape((-1,) + (1,) * (len(dims) - 1 - dim))
    return factor_of


def deal_out(own_key, own, number, rows, count, top, reach, skew):
    order = jax.random.permutation(own_key, count)
    packed, common = load_shares(count, rows * top, reach, skew, True), load_shares(count, rows * top, reach, skew, False)
    places = jnp.arange(count)

    def named(lengths, offset_by):
        used = int((lengths > 0).sum())
        fixed = max(1, used // 4)
        shifted = fixed + (places - fixed + offset_by * (used - fixed)) % max(1, count - fixed)
        return jnp.zeros((count,), jnp.int32).at[order[jnp.where(places < fixed, places, shifted)]].set(jnp.asarray(lengths, jnp.int32))

    lengths = jnp.where(number % 4 == 0, named(packed, number // 4), named(common, number - number // 4 - 1))
    mixed = jax.random.permutation(jax.random.fold_in(own, 3), count)
    donor, taker = mixed[0:count // 2 * 2:2], mixed[1:count // 2 * 2:2]
    room = jnp.minimum(lengths[donor] - 1, reach - lengths[taker]) // 2
    room = jnp.where((donor == order[0]) | (taker == order[0]) | (lengths[taker] == 0), 0, jnp.maximum(room, 0))
    shifted = jax.random.randint(jax.random.fold_in(own, 4), (count // 2,), 0, 1 << 20) % (room + 1)
    lengths = lengths.at[donor].add(-shifted).at[taker].add(shifted)
    labels = jnp.searchsorted(jnp.cumsum(lengths), jnp.arange(rows * top), side="right").astype(jnp.int32)
    table = labels.reshape(top, rows).T
    table = table[jax.random.permutation(jax.random.fold_in(own, 1), rows)]
    offset_by = jax.random.randint(jax.random.fold_in(own, 2), (rows, 1), 0, top)
    return jnp.take_along_axis(table, (jnp.arange(top)[None, :] + offset_by) % top, axis=1)


def load_shares(count, total, limit, skew, full):
    weights = [(1 << 20) // math.isqrt(rank ** skew) + 1 for rank in range(1, count + 1)]
    largest = limit if full else min(limit, max(-(-total // count), total * weights[0] // sum(weights)))
    least = 1 if total - largest >= count - 1 else 0
    holding, surplus = [largest] + [least] * (count - 1), total - largest - least * (count - 1)
    while surplus > 0:
        free = [i for i in range(1, count) if holding[i] < largest] or [i for i in range(1, count) if holding[i] < limit]
        whole, remaining = sum([weights[i] for i in free]), surplus
        for i in free:
            more = min(limit - holding[i], max(1, remaining * weights[i] // whole), surplus)
            holding[i] = holding[i] + more
            surplus = surplus - more
    return np.array(holding)


def scatter_about(stream_key, extent, scale, most, split=(), dtype=jnp.bfloat16):
    factor_of = block_levels(stream_key, extent, split, -0.22, 0.18) if split else 1.0
    array = jax.random.normal(stream_key, extent, jnp.float32) * scale * factor_of
    return jnp.minimum(jnp.maximum(array, -most), most).astype(dtype)


def gaussian_with(key, extent, width, reach, split, heavy, held_as=jnp.bfloat16):
    values = width * jax.random.normal(key, extent, jnp.float32)
    if split:
        values = values * block_levels(key, extent, split, -0.22, 0.18)
    return jnp.clip(raised(values, jax.random.fold_in(key, 3), *heavy), -reach, reach).astype(held_as)


def setup_inputs(seed: int = 0) -> dict:
    seeds = jax.random.split(jax.random.key(seed), 7)
    tokens = scatter_about(seeds[0], (STEPS, ROWS, D), 1.0, 6.0, ((1, 4), (2, 32)))
    expert_ids_keys = jax.random.split(jax.random.fold_in(seeds[1], 1), STEPS * ROWS // ROW_DEV)
    expert_ids_turns = jax.random.permutation(jax.random.fold_in(seeds[1], 3), STEPS * ROWS // ROW_DEV)
    expert_ids = jax.vmap(lambda own, number: deal_out(jax.random.fold_in(seeds[1], 2), own, number, ROW_DEV, EXPERTS, 2, ROW_DEV, 2))(expert_ids_keys, expert_ids_turns).reshape((STEPS, ROWS, 2))
    route_share = jnp.clip(0.1 + 0.79999997 * jax.random.uniform(seeds[2], (STEPS, ROWS), jnp.float32) ** block_levels(seeds[2], (STEPS, ROWS), ((1, 4),), -0.2, 0.2), 0.1, 0.9)
    gate_weight = scatter_about(seeds[3], (EXPERTS, D, FF), D ** -0.5, 0.078125, ((0, 4), (2, 32)))
    up_weight = scatter_about(seeds[4], (EXPERTS, D, FF), D ** -0.5, 0.078125, ((0, 4), (2, 32)))
    down_weight = gaussian_with(seeds[5], (EXPERTS, FF, D), FF ** -0.5, 0.09375, ((0, 4), (1, 32)), (1, 2, 32, 2.75))
    return dict(tokens=tokens, expert_ids=expert_ids, route_share=route_share, gate_weight=gate_weight, up_weight=up_weight, down_weight=down_weight)


def reference(tokens, expert_ids, route_share, gate_weight, up_weight, down_weight):
    block_width = FF // N_BLK
    results = []
    for step_idx in range(STEPS):
        step_rows = tokens[step_idx]
        share_now = route_share[step_idx]
        running = jnp.zeros((ROWS, D), jnp.float32)
        for expert_idx in range(EXPERTS):
            gate_pre = jnp.dot(step_rows, gate_weight[expert_idx], preferred_element_type=jnp.float32)
            up_pre = jnp.dot(step_rows, up_weight[expert_idx], preferred_element_type=jnp.float32)
            hidden = (jax.nn.silu(gate_pre) * up_pre).astype(jnp.bfloat16)
            accumulated = jnp.zeros((ROWS, D), jnp.float32)
            for block_idx in range(N_BLK):
                lower = block_idx * block_width
                partial_value = jnp.dot(hidden[:, lower:lower + block_width], down_weight[expert_idx, lower:lower + block_width], preferred_element_type=jnp.float32)
                partial_value = lax.optimization_barrier(partial_value.astype(jnp.bfloat16))
                accumulated = accumulated + partial_value.astype(jnp.float32)
            expert_out = lax.optimization_barrier(accumulated.astype(jnp.bfloat16)).astype(jnp.float32)
            factor = jnp.where(expert_ids[step_idx, :, 0] == expert_idx, share_now, jnp.zeros_like(share_now))
            factor = factor + jnp.where(expert_ids[step_idx, :, 1] == expert_idx, 1.0 - share_now, jnp.zeros_like(share_now))
            running = running + factor[:, None] * expert_out
        results.append(running.astype(jnp.bfloat16))
    return jnp.stack(results)
```

```python
import jax
import jax.numpy as jnp
from jax import lax
from jax.experimental import pallas as pl
from jax.experimental.pallas import tpu as pltpu
from jax.sharding import PartitionSpec as P

SIDE = 4
BF = jnp.bfloat16
F32 = jnp.float32


def blk_perm(bulk, shift):
    pairs = []
    for z in range(SIDE):
        for x in range(SIDE):
            for c in range(2):
                along_z = (c == 0) == bulk
                z2 = (z + shift) % SIDE if along_z else z
                x2 = x if along_z else (x + shift) % SIDE
                pairs.append(((z * SIDE + x) * 2 + c, (z2 * SIDE + x2) * 2 + c))
    return pairs


def move_bulk(v, shift):
    return lax.ppermute(v, "blk", blk_perm(True, shift))


def move_small(v, shift):
    return lax.ppermute(v, "blk", blk_perm(False, shift))


def move_core(v):
    return lax.ppermute(v, "blk", [(i, i ^ 1) for i in range(2 * SIDE * SIDE)])


def move_expert(v, shift):
    return lax.ppermute(v, "expert", [(i, (i + shift) % SIDE) for i in range(SIDE)])


def feature_block(z, x, core, bulk_shift, small_shift):
    along_z = jnp.where(core == 0, bulk_shift, small_shift)
    along_x = jnp.where(core == 0, small_shift, bulk_shift)
    return ((z + along_z) % SIDE) * SIDE + (x + along_x) % SIDE


def up_call(pieces, idx, gate_w, up_w, carry, final):
    n = len(pieces)
    rows, width = pieces[0].shape[1:]
    cols = gate_w.shape[1]
    tile = 256

    def kernel(idx_ref, *refs):
        xs = refs[:n]
        ws = refs[n : n + 8 * n]
        rest = refs[n + 8 * n :]
        x = jnp.concatenate([r[k] for r in xs for k in range(SIDE)], axis=1)
        g = jnp.dot(x, jnp.concatenate([w[...] for w in ws[: 4 * n]], axis=0), preferred_element_type=F32)
        u = jnp.dot(x, jnp.concatenate([w[...] for w in ws[4 * n :]], axis=0), preferred_element_type=F32)
        if carry is not None:
            g = g + rest[0][...]
            u = u + rest[1][...]
            rest = rest[2:]
        if final:
            rest[0][...] = (g / (1.0 + jnp.exp(-g)) * u).astype(BF)
        else:
            rest[0][...] = g
            rest[1][...] = u

    def wspec(k):
        return pl.BlockSpec((width, tile), lambda j, idx_ref: (idx_ref[k], j))

    out_spec = pl.BlockSpec((rows, tile), lambda j, idx_ref: (0, j))
    in_specs = [pl.BlockSpec((SIDE, rows, width), lambda j, idx_ref: (0, 0, 0))] * n
    in_specs += [wspec(k) for k in range(4 * n)] * 2
    args = [*pieces, *([gate_w] * (4 * n)), *([up_w] * (4 * n))]
    if carry is not None:
        in_specs += [out_spec] * 2
        args += list(carry)
    if final:
        out_shape = jax.ShapeDtypeStruct((rows, cols), BF)
        out_specs = out_spec
    else:
        out_shape = [jax.ShapeDtypeStruct((rows, cols), F32)] * 2
        out_specs = [out_spec] * 2
    return pl.pallas_call(
        kernel,
        grid_spec=pltpu.PrefetchScalarGridSpec(
            num_scalar_prefetch=1, grid=(cols // tile,), in_specs=in_specs, out_specs=out_specs
        ),
        out_shape=out_shape,
        compiler_params=pltpu.CompilerParams(vmem_limit_bytes=24 << 20),
        cost_estimate=pl.CostEstimate(
            flops=2 * rows * 4 * n * width * cols * 2,
            bytes_accessed=4 * n * width * cols * 4 + n * 4 * rows * width * 2 + rows * cols * 8,
            transcendentals=0,
        ),
        name="up",
    )(idx, *args)


def down_call(hidden, idx, down_w, add):
    rows, depth = hidden.shape
    width = down_w.shape[1] // (SIDE * SIDE)

    def kernel(idx_ref, h_ref, w0, w1, *rest):
        y = jnp.dot(h_ref[...], jnp.concatenate([w0[...], w1[...]], axis=1), preferred_element_type=F32)
        for k in range(2):
            part = y[:, k * width : (k + 1) * width]
            if add is not None:
                part = part + rest[0][k].astype(F32)
            rest[-1][k] = part.astype(BF)

    block = pl.BlockSpec((2, rows, width), lambda j, idx_ref: (j, 0, 0))
    in_specs = [
        pl.BlockSpec((rows, depth), lambda j, idx_ref: (0, 0)),
        pl.BlockSpec((depth, width), lambda j, idx_ref: (0, idx_ref[2 * j])),
        pl.BlockSpec((depth, width), lambda j, idx_ref: (0, idx_ref[2 * j + 1])),
    ]
    args = [hidden, down_w, down_w]
    if add is not None:
        in_specs.append(block)
        args.append(add)
    return pl.pallas_call(
        kernel,
        grid_spec=pltpu.PrefetchScalarGridSpec(
            num_scalar_prefetch=1, grid=(SIDE // 2,), in_specs=in_specs, out_specs=block
        ),
        out_shape=jax.ShapeDtypeStruct((SIDE, rows, width), BF),
        compiler_params=pltpu.CompilerParams(vmem_limit_bytes=16 << 20),
        cost_estimate=pl.CostEstimate(
            flops=2 * rows * depth * width * SIDE,
            bytes_accessed=SIDE * width * (depth + rows * 2) * 2 + rows * depth * 2,
            transcendentals=0,
        ),
        name="down",
    )(idx, *args)


def fsum(parts):
    total = parts[0].astype(F32)
    for p in parts[1:]:
        total = total + p.astype(F32)
    return total


def body(tokens, expert_ids, route_share, gate_weight, up_weight, down_weight):
    expert = lax.axis_index("expert")
    place = lax.axis_index("blk")
    z, x, c = place // (2 * SIDE), (place // 2) % SIDE, place % 2
    gate_w, up_w, down_w = gate_weight[0], up_weight[0], down_weight[0]
    half = tokens.shape[2]
    rows = tokens.shape[1]

    mine = jnp.where(c == 0, tokens[0], tokens[1])
    theirs = jnp.where(c == 0, tokens[1], tokens[0])
    got = move_core(theirs)
    pair = jnp.where(
        c == 0, jnp.concatenate([mine, got], axis=1), jnp.concatenate([got, mine], axis=1)
    )
    owners = jnp.concatenate([pair] + [move_expert(pair, d) for d in range(1, SIDE)], axis=0)
    line = jnp.stack([owners] + [move_small(owners, d) for d in range(1, SIDE)])
    own = {0: line}
    for d in (1, 3, 2):
        own[d] = move_bulk(line, d)
    other = {d: move_core(own[d]) for d in (0, 1, 3, 2)}

    def idx_in(core, d):
        return jnp.stack([feature_block(z, x, core, -d, -k) for k in range(SIDE)]).astype(jnp.int32)

    def idx_out(core, d):
        return jnp.stack([feature_block(z, x, core, d, k) for k in range(SIDE)]).astype(jnp.int32)

    hidden = []
    carry_own = carry_other = None
    for d in (0, 1, 3, 2):
        carry_own = up_call([own[d]], idx_in(c, d), gate_w, up_w, carry_own, d == 2)
        carry_other = up_call([other[d]], idx_in(1 - c, d), gate_w, up_w, carry_other, d == 2)
    h_own, h_other = carry_own, carry_other

    merged = {}
    for d in (2, 1, 3, 0):
        sent = move_core(down_call(h_own, idx_out(1 - c, d), down_w, None))
        merged[d] = down_call(h_other, idx_out(c, d), down_w, sent)
    line_sum = fsum([merged[0]] + [move_bulk(merged[d], d) for d in (1, 3, 2)]).astype(BF)
    plane = fsum([line_sum[0]] + [move_small(line_sum[k], k) for k in (1, 3, 2)]).astype(BF)
    plane = plane.reshape(SIDE, rows, 2 * half)

    ids = jnp.where(c == 0, expert_ids[1], expert_ids[0])
    share = jnp.where(c == 0, route_share[1], route_share[0])
    total = 0.0
    for d in range(SIDE):
        back = plane[d] if d == 0 else move_expert(plane[d], -d)
        named = (expert + d) % SIDE
        factor = jnp.where(ids[:, 0] == named, share, 0.0) + jnp.where(ids[:, 1] == named, 1.0 - share, 0.0)
        total = total + factor[:, None] * back.astype(F32)
    total = total.astype(BF)
    low, high = total[:, :half], total[:, half:]
    keep = jnp.where(c == 0, low, high)
    came = move_core(jnp.where(c == 0, high, low))
    return jnp.stack([jnp.where(c == 0, came, keep), jnp.where(c == 0, keep, came)])


def solution(mesh):
    return jax.shard_map(
        body,
        mesh=mesh,
        in_specs=(
            P(None, "expert", "blk"),
            P(None, "expert", None),
            P(None, "expert"),
            P("expert", None, "blk"),
            P("expert", None, "blk"),
            P("expert", "blk", None),
        ),
        out_specs=P(None, "expert", "blk"),
        check_vma=False,
    )
```

```python
import jax
import jax.numpy as jnp
from jax import lax
from jax.experimental import pallas as pl
from jax.experimental.pallas import tpu as pltpu
from jax.sharding import PartitionSpec as P

SIDE = 4
BF = jnp.bfloat16
F32 = jnp.float32


def blk_perm(bulk, shift):
    pairs = []
    for z in range(SIDE):
        for x in range(SIDE):
            for c in range(2):
                along_z = (c == 0) == bulk
                z2 = (z + shift) % SIDE if along_z else z
                x2 = x if along_z else (x + shift) % SIDE
                pairs.append(((z * SIDE + x) * 2 + c, (z2 * SIDE + x2) * 2 + c))
    return pairs


def move_bulk(v, shift):
    return lax.ppermute(v, "blk", blk_perm(True, shift))


def move_small(v, shift):
    return lax.ppermute(v, "blk", blk_perm(False, shift))


def move_core(v):
    return lax.ppermute(v, "blk", [(i, i ^ 1) for i in range(2 * SIDE * SIDE)])


def move_expert(v, shift):
    return lax.ppermute(v, "expert", [(i, (i + shift) % SIDE) for i in range(SIDE)])


def feature_block(place, sign, other, bulk_shift, small_shift):
    z, x, core = place >> 3, (place >> 1) & (SIDE - 1), (place & 1) ^ other
    along_z = jnp.where(core == 0, sign * bulk_shift, sign * small_shift)
    along_x = jnp.where(core == 0, sign * small_shift, sign * bulk_shift)
    return ((z + along_z) & (SIDE - 1)) * SIDE + ((x + along_x) & (SIDE - 1))


def after(value, *others):
    return lax.optimization_barrier((value, *others))[0]


VMEM = pl.BlockSpec(memory_space=pltpu.VMEM)
SMEM = pl.BlockSpec(memory_space=pltpu.SMEM)
ANY = pl.BlockSpec(memory_space=pl.ANY)


def in_vmem(values):
    return [pltpu.with_memory_space_constraint(v, pltpu.VMEM) for v in values]


def up_call(pieces, place, blocks, gate_w, up_w, carry, final, behind):
    n = len(pieces)
    counts = [p.shape[0] for p in pieces]
    total = sum(counts)
    rows, width = pieces[0].shape[1:]
    cols = gate_w.shape[1]
    tile = 256

    def kernel(place_ref, *refs):
        xs = refs[:n]
        gate_ref, up_ref = refs[n : n + 2]
        rest = refs[n + 2 :]
        carried = rest[:2] if carry is not None else None
        outs = rest[(2 if carry is not None else 0) + len(behind) :]
        outs[-1][...] = jnp.zeros((8, 128), F32)
        x = jnp.concatenate([r[k] for r, m in zip(xs, counts) for k in range(m)], axis=1)
        at = [pl.multiple_of(feature_block(place_ref[0], *b) * width, width) for b in blocks]
        for j in range(cols // tile):
            cs = slice(j * tile, (j + 1) * tile)
            g = jnp.dot(x, jnp.concatenate([gate_ref[pl.ds(s, width), cs] for s in at], axis=0), preferred_element_type=F32)
            u = jnp.dot(x, jnp.concatenate([up_ref[pl.ds(s, width), cs] for s in at], axis=0), preferred_element_type=F32)
            if carried is not None:
                g = g + carried[0][:, cs]
                u = u + carried[1][:, cs]
            if final:
                outs[0][:, cs] = (g / (1.0 + jnp.exp(-g)) * u).astype(BF)
            else:
                outs[0][:, cs] = g
                outs[1][:, cs] = u

    args = in_vmem([*pieces, gate_w, up_w, *(carry or [])])
    if final:
        out_shape = [pltpu.VMEM((rows, cols), BF)]
    else:
        out_shape = [pltpu.VMEM((rows, cols), F32)] * 2
    out_shape.append(pltpu.VMEM((8, 128), F32))
    return pl.pallas_call(
        kernel,
        in_specs=[SMEM] + [VMEM] * len(args) + [ANY] * len(behind),
        out_specs=[VMEM] * len(out_shape),
        out_shape=out_shape,
        compiler_params=pltpu.CompilerParams(vmem_limit_bytes=12 << 20),
        cost_estimate=pl.CostEstimate(
            flops=2 * rows * total * width * cols * 2,
            bytes_accessed=total * width * cols * 4 + total * rows * width * 2 + rows * cols * 8,
            transcendentals=0,
        ),
        name="up",
    )(place, *args, *behind)


def down_call(hidden, place, blocks, down_w, adds, splits, dtype, behind):
    rows, depth = hidden.shape
    width = down_w.shape[1] // (SIDE * SIDE)
    n_add = len(adds)
    total = len(blocks)

    def kernel(place_ref, h_ref, w_ref, *rest):
        outs = [(o, k) for o, n in zip(rest[n_add + len(behind) :], splits) for k in range(n)]
        h = h_ref[...]
        for j in range(0, total, 2):
            at = [pl.multiple_of(feature_block(place_ref[0], *b) * width, width) for b in blocks[j : j + 2]]
            w = jnp.concatenate([w_ref[:, pl.ds(s, width)] for s in at], axis=1)
            y = jnp.dot(h, w, preferred_element_type=F32)
            for k in range(2):
                part = y[:, k * width : (k + 1) * width]
                for ref, (_, first) in zip(rest, adds):
                    part = part + ref[j + k + first].astype(F32)
                out, place = outs[j + k]
                out[place] = part.astype(dtype)

    args = in_vmem([hidden, down_w, *[v for v, _ in adds]])
    out_shape = [pltpu.VMEM((n, rows, width), dtype) for n in splits]
    return pl.pallas_call(
        kernel,
        in_specs=[SMEM] + [VMEM] * len(args) + [ANY] * len(behind),
        out_specs=[VMEM] * len(out_shape),
        out_shape=out_shape,
        compiler_params=pltpu.CompilerParams(vmem_limit_bytes=12 << 20),
        cost_estimate=pl.CostEstimate(
            flops=2 * rows * depth * width * total,
            bytes_accessed=total * width * (depth + rows * 2) * 2 + rows * depth * 2,
            transcendentals=0,
        ),
        name="down",
    )(place, *args, *behind)


def load_call(weights, behind):
    n = len(weights)

    def kernel(*refs):
        sem = refs[-1]
        refs[-2][...] = jnp.zeros((8, 128), F32)
        copies = [pltpu.make_async_copy(refs[k], refs[n + len(behind) + k], sem.at[k]) for k in range(n)]
        for copy in copies:
            copy.start()
        for copy in copies:
            copy.wait()

    return pl.pallas_call(
        kernel,
        in_specs=[pl.BlockSpec(memory_space=pltpu.HBM)] * n + [ANY] * len(behind),
        out_specs=[VMEM] * (n + 1),
        out_shape=[pltpu.VMEM(w.shape, w.dtype) for w in weights] + [pltpu.VMEM((8, 128), F32)],
        scratch_shapes=[pltpu.SemaphoreType.DMA((n,))],
        compiler_params=pltpu.CompilerParams(vmem_limit_bytes=1 << 20),
        cost_estimate=pl.CostEstimate(
            flops=0, bytes_accessed=4 * sum(w.size for w in weights), transcendentals=0
        ),
        name="load",
    )(*[pltpu.with_memory_space_constraint(w, pltpu.HBM) for w in weights], *behind)


def gather_call(pieces, out_shapes, places, behind):
    n = len(pieces)

    def kernel(*refs):
        for ref, (k, index) in zip(refs[:n], places):
            refs[n + 1 + k][index] = ref[...]

    return pl.pallas_call(
        kernel,
        in_specs=[VMEM] * n + [ANY],
        out_specs=[VMEM] * len(out_shapes),
        out_shape=[pltpu.VMEM(shape, BF) for shape in out_shapes],
        compiler_params=pltpu.CompilerParams(vmem_limit_bytes=8 << 20),
        cost_estimate=pl.CostEstimate(
            flops=0, bytes_accessed=4 * sum(p.size for p in pieces), transcendentals=0
        ),
        name="gather",
    )(*in_vmem(pieces), behind)


def add_call(total, arrived):
    n = total.shape[0]

    def kernel(total_ref, arrived_ref, *outs):
        for k in range(n):
            outs[k][...] = (total_ref[k] + arrived_ref[k].astype(F32)).astype(BF)

    return pl.pallas_call(
        kernel,
        in_specs=[VMEM] * 2,
        out_specs=[VMEM] * n,
        out_shape=[pltpu.VMEM(total.shape[1:], BF)] * n,
        compiler_params=pltpu.CompilerParams(vmem_limit_bytes=8 << 20),
        cost_estimate=pl.CostEstimate(flops=total.size, bytes_accessed=8 * total.size, transcendentals=0),
        name="add",
    )(*in_vmem([total, arrived]))


def fsum(parts):
    total = parts[0].astype(F32)
    for p in parts[1:]:
        total = total + p.astype(F32)
    return total


def body(tokens, expert_ids, route_share, gate_weight, up_weight, down_weight):
    expert = lax.axis_index("expert")
    place = lax.axis_index("blk")
    where = jnp.reshape(place, (1,))
    tokens, where = lax.optimization_barrier((tokens, where))
    c = place % 2
    gate_w, up_w, down_w = gate_weight[0], up_weight[0], down_weight[0]
    half = tokens.shape[2]
    rows = tokens.shape[1]

    mine = jnp.where(c == 0, tokens[0], tokens[1])
    theirs = jnp.where(c == 0, tokens[1], tokens[0])
    got = move_core(theirs)
    pair = jnp.where(
        c == 0, jnp.concatenate([mine, got], axis=1), jnp.concatenate([got, mine], axis=1)
    )
    two = SIDE // 2
    ids = jnp.where(c == 0, expert_ids[1], expert_ids[0])
    share = jnp.where(c == 0, route_share[1], route_share[0])
    names = (expert + jnp.arange(SIDE, dtype=jnp.int32)) % SIDE
    factors = jnp.where(ids[:, 0] == names[:, None], share, 0.0) + jnp.where(ids[:, 1] == names[:, None], 1.0 - share, 0.0)
    gate_w, up_w, t0 = load_call([gate_w, up_w], [pair, factors])
    (owners,) = gather_call(
        [pair] + [move_expert(pair, d) for d in range(1, SIDE)],
        [(SIDE * rows, 2 * half)],
        [(0, slice(d * rows, (d + 1) * rows)) for d in range(SIDE)],
        t0,
    )
    down_w, t1 = load_call([down_w], [owners])
    line_a, line_b = gather_call(
        [owners] + [move_small(owners, d) for d in range(1, SIDE)],
        [(two, SIDE * rows, 2 * half)] * 2,
        [(d // two, d % two) for d in range(SIDE)],
        t1,
    )
    def at(sign, other, d, blocks=range(SIDE)):
        return [(sign, other, d, k) for k in blocks]

    first, last = range(two), range(two, SIDE)

    def up(pieces, blocks, carry, final=False, behind=()):
        *sums, token = up_call(pieces, where, blocks, gate_w, up_w, carry, final, behind)
        return sums, token

    def down(h, blocks, adds, splits, dtype=BF, behind=()):
        return down_call(h, where, blocks, down_w, adds, splits, dtype, behind)

    right_a, left_b = move_bulk(line_a, 1), move_bulk(line_b, 3)
    right_b, left_a = move_bulk(line_b, 1), move_bulk(line_a, 3)
    far_a, far_b = move_bulk(right_a, 1), move_bulk(left_b, 3)
    other_line = [move_core(line_a), move_core(line_b)]
    other_early = [move_core(right_a), move_core(left_b)]
    own_sum, t0 = up([line_a, line_b], at(-1, 0, 0), None)
    other_sum, t1 = up(other_line, at(-1, 1, 0), None, False, [t0])
    early = [(1, first), (3, last)]
    late = [(1, last), (3, first)]

    def near(other, parts):
        return [b for d, blocks in parts for b in at(-1, other, d, blocks)]

    other_sum, t1 = up(other_early, near(1, early), other_sum)
    right_b, left_a = after(right_b, t1), after(left_a, t1)
    other_late = [move_core(right_b), move_core(left_a)]
    own_sum, t0 = up([right_a, left_b, right_b, left_a], near(0, early + late), own_sum)
    other_sum, t1 = up(other_late, near(1, late), other_sum, False, [t0])
    far_a, far_b = after(far_a, t1), after(far_b, t1)
    other_a, other_b = move_core(far_a), move_core(far_b)
    (h_own,), t0 = up([far_a, far_b], at(-1, 0, 2), own_sum, True)

    sent2 = move_core(down(h_own, at(1, 1, 2), [], [SIDE])[0])
    (h_other,), t1 = up([other_a, other_b], at(-1, 1, 2), other_sum, True)
    m2a, m2b = down(h_other, at(1, 0, 2), [(sent2, 0)], [two, two])
    step_a, step_b = move_bulk(m2a, 1), move_bulk(m2b, 3)
    sent1 = move_core(down(h_own, at(1, 1, 1), [], [SIDE], BF, [m2a])[0])
    sent3 = move_core(down(h_own, at(1, 1, 3), [], [SIDE], BF, [m2a])[0])
    (m1b,) = down(h_other, at(1, 0, 1, last), [(sent1, two)], [two])
    (m3a,) = down(h_other, at(1, 0, 3, first), [(sent3, 0)], [two])
    n1b, n3a = move_bulk(m1b, 1), move_bulk(m3a, 3)
    sent0 = move_core(down(h_own, at(1, 1, 0), [], [SIDE], BF, [m1b, m3a])[0])
    step_a, step_b = after(step_a, m1b, m3a), after(step_b, m1b, m3a)
    (m1a,) = down(h_other, at(1, 0, 1, first), [(sent1, 0), (step_a, 0)], [two])
    (m3b,) = down(h_other, at(1, 0, 3, last), [(sent3, two), (step_b, 0)], [two])
    n1a, n3b = move_bulk(m1a, 1), move_bulk(m3b, 3)
    (m0a,) = down(h_other, at(1, 0, 0, first), [(sent0, 0), (n3a, 0)], [two], F32, [m1a, m3b])
    (m0b,) = down(h_other, at(1, 0, 0, last), [(sent0, two), (n1b, 0)], [two], F32, [m1a, m3b])
    s0, s1 = add_call(m0a, n1a)
    s2, s3 = add_call(m0b, n3b)
    plane = fsum([s0, move_small(s1, 1), move_small(s3, 3), move_small(s2, 2)]).astype(BF)
    plane = plane.reshape(SIDE, rows, 2 * half)

    total = 0.0
    for d in range(SIDE):
        back = plane[d] if d == 0 else move_expert(plane[d], -d)
        total = total + factors[d][:, None] * back.astype(F32)
    total = total.astype(BF)
    low, high = total[:, :half], total[:, half:]
    keep = jnp.where(c == 0, low, high)
    came = move_core(jnp.where(c == 0, high, low))
    return jnp.stack([jnp.where(c == 0, came, keep), jnp.where(c == 0, keep, came)])


def solution(mesh):
    return jax.shard_map(
        body,
        mesh=mesh,
        in_specs=(
            P(None, "expert", "blk"),
            P(None, "expert", None),
            P(None, "expert"),
            P("expert", None, "blk"),
            P("expert", None, "blk"),
            P("expert", "blk", None),
        ),
        out_specs=P(None, "expert", "blk"),
        check_vma=False,
    )
```

```python
import jax
import jax.numpy as jnp
from jax import lax
from jax.experimental import pallas as pl
from jax.experimental.pallas import tpu as pltpu
from jax.sharding import PartitionSpec as P

SIDE = 4
FAR_FIRST = (2, 1, 3)
BF = jnp.bfloat16
F32 = jnp.float32


def blk_perm(bulk, shift):
    pairs = []
    for z in range(SIDE):
        for x in range(SIDE):
            for c in range(2):
                along_z = (c == 0) == bulk
                z2 = (z + shift) % SIDE if along_z else z
                x2 = x if along_z else (x + shift) % SIDE
                pairs.append(((z * SIDE + x) * 2 + c, (z2 * SIDE + x2) * 2 + c))
    return pairs


def move_bulk(v, shift):
    return lax.ppermute(v, "blk", blk_perm(True, shift))


def move_small(v, shift):
    return lax.ppermute(v, "blk", blk_perm(False, shift))


def move_core(v):
    return lax.ppermute(v, "blk", [(i, i ^ 1) for i in range(2 * SIDE * SIDE)])


def move_expert(v, shift):
    return lax.ppermute(v, "expert", [(i, (i + shift) % SIDE) for i in range(SIDE)])


def feature_block(place, sign, other, bulk_shift, small_shift):
    z, x, core = place >> 3, (place >> 1) & (SIDE - 1), (place & 1) ^ other
    along_z = jnp.where(core == 0, sign * bulk_shift, sign * small_shift)
    along_x = jnp.where(core == 0, sign * small_shift, sign * bulk_shift)
    return ((z + along_z) & (SIDE - 1)) * SIDE + ((x + along_x) & (SIDE - 1))


def after(value, *others):
    return lax.optimization_barrier((value, *others))[0]


VMEM = pl.BlockSpec(memory_space=pltpu.VMEM)
SMEM = pl.BlockSpec(memory_space=pltpu.SMEM)
ANY = pl.BlockSpec(memory_space=pl.ANY)


def in_vmem(values):
    return [pltpu.with_memory_space_constraint(v, pltpu.VMEM) for v in values]


def up_call(pieces, place, blocks, gate_w, up_w, carry, final, behind):
    n = len(pieces)
    counts = [p.shape[0] for p in pieces]
    total = sum(counts)
    rows, width = pieces[0].shape[1:]
    cols = gate_w.shape[1]
    tile = 256

    def kernel(place_ref, *refs):
        xs = refs[:n]
        gate_ref, up_ref = refs[n : n + 2]
        rest = refs[n + 2 :]
        carried = rest[:2] if carry is not None else None
        outs = rest[(2 if carry is not None else 0) + len(behind) :]
        outs[-1][...] = jnp.zeros((8, 128), F32)
        x = jnp.concatenate([r[k] for r, m in zip(xs, counts) for k in range(m)], axis=1)
        at = [pl.multiple_of(feature_block(place_ref[0], *b) * width, width) for b in blocks]
        for j in range(cols // tile):
            cs = slice(j * tile, (j + 1) * tile)
            g = jnp.dot(x, jnp.concatenate([gate_ref[pl.ds(s, width), cs] for s in at], axis=0), preferred_element_type=F32)
            u = jnp.dot(x, jnp.concatenate([up_ref[pl.ds(s, width), cs] for s in at], axis=0), preferred_element_type=F32)
            if carried is not None:
                g = g + carried[0][:, cs]
                u = u + carried[1][:, cs]
            if final:
                outs[0][:, cs] = (g / (1.0 + jnp.exp(-g)) * u).astype(BF)
            else:
                outs[0][:, cs] = g
                outs[1][:, cs] = u

    args = in_vmem([*pieces, gate_w, up_w, *(carry or [])])
    if final:
        out_shape = [pltpu.VMEM((rows, cols), BF)]
    else:
        out_shape = [pltpu.VMEM((rows, cols), F32)] * 2
    out_shape.append(pltpu.VMEM((8, 128), F32))
    return pl.pallas_call(
        kernel,
        in_specs=[SMEM] + [VMEM] * len(args) + [ANY] * len(behind),
        out_specs=[VMEM] * len(out_shape),
        out_shape=out_shape,
        compiler_params=pltpu.CompilerParams(vmem_limit_bytes=12 << 20),
        cost_estimate=pl.CostEstimate(
            flops=2 * rows * total * width * cols * 2,
            bytes_accessed=total * width * cols * 4 + total * rows * width * 2 + rows * cols * 8,
            transcendentals=0,
        ),
        name="up",
    )(place, *args, *behind)


def down_call(hidden, place, blocks, down_w, adds, splits, dtype, behind):
    rows, depth = hidden.shape
    width = down_w.shape[1] // (SIDE * SIDE)
    n_add = len(adds)
    total = len(blocks)

    def kernel(place_ref, h_ref, w_ref, *rest):
        outs = [(o, k) for o, n in zip(rest[n_add + len(behind) :], splits) for k in range(n)]
        h = h_ref[...]
        for j in range(0, total, 2):
            at = [pl.multiple_of(feature_block(place_ref[0], *b) * width, width) for b in blocks[j : j + 2]]
            w = jnp.concatenate([w_ref[:, pl.ds(s, width)] for s in at], axis=1)
            y = jnp.dot(h, w, preferred_element_type=F32)
            for k in range(len(at)):
                part = y[:, k * width : (k + 1) * width]
                for ref, (v, first) in zip(rest, adds):
                    if 0 <= j + k + first < v.shape[0]:
                        part = part + ref[j + k + first].astype(F32)
                out, place = outs[j + k]
                out[place] = part.astype(dtype)

    args = in_vmem([hidden, down_w, *[v for v, _ in adds]])
    out_shape = [pltpu.VMEM((n, rows, width), dtype) for n in splits]
    return pl.pallas_call(
        kernel,
        in_specs=[SMEM] + [VMEM] * len(args) + [ANY] * len(behind),
        out_specs=[VMEM] * len(out_shape),
        out_shape=out_shape,
        compiler_params=pltpu.CompilerParams(vmem_limit_bytes=12 << 20),
        cost_estimate=pl.CostEstimate(
            flops=2 * rows * depth * width * total,
            bytes_accessed=total * width * (depth + rows * 2) * 2 + rows * depth * 2,
            transcendentals=0,
        ),
        name="down",
    )(place, *args, *behind)


def load_call(weights, behind):
    n = len(weights)

    def kernel(*refs):
        sem = refs[-1]
        refs[-2][...] = jnp.zeros((8, 128), F32)
        copies = [pltpu.make_async_copy(refs[k], refs[n + len(behind) + k], sem.at[k]) for k in range(n)]
        for copy in copies:
            copy.start()
        for copy in copies:
            copy.wait()

    return pl.pallas_call(
        kernel,
        in_specs=[pl.BlockSpec(memory_space=pltpu.HBM)] * n + [ANY] * len(behind),
        out_specs=[VMEM] * (n + 1),
        out_shape=[pltpu.VMEM(w.shape, w.dtype) for w in weights] + [pltpu.VMEM((8, 128), F32)],
        scratch_shapes=[pltpu.SemaphoreType.DMA((n,))],
        compiler_params=pltpu.CompilerParams(vmem_limit_bytes=1 << 20),
        cost_estimate=pl.CostEstimate(
            flops=0, bytes_accessed=4 * sum(w.size for w in weights), transcendentals=0
        ),
        name="load",
    )(*[pltpu.with_memory_space_constraint(w, pltpu.HBM) for w in weights], *behind)


def gather_call(pieces, out_shapes, places, behind):
    n = len(pieces)

    def kernel(*refs):
        for ref, to in zip(refs[:n], places):
            for k, index, part in to:
                refs[n + len(behind) + k][index] = ref[part]

    return pl.pallas_call(
        kernel,
        in_specs=[VMEM] * n + [ANY] * len(behind),
        out_specs=[VMEM] * len(out_shapes),
        out_shape=[pltpu.VMEM(shape, BF) for shape in out_shapes],
        compiler_params=pltpu.CompilerParams(vmem_limit_bytes=8 << 20),
        cost_estimate=pl.CostEstimate(
            flops=0, bytes_accessed=4 * sum(p.size for p in pieces), transcendentals=0
        ),
        name="gather",
    )(*in_vmem(pieces), *behind)


def add_call(total, *arrived):
    n = total.shape[0]

    def kernel(total_ref, *refs):
        for k in range(n):
            out = total_ref[k]
            for ref in refs[: len(arrived)]:
                out = out + ref[k].astype(F32)
            refs[len(arrived) + k][...] = out.astype(BF)

    args = in_vmem([total, *arrived])
    return pl.pallas_call(
        kernel,
        in_specs=[VMEM] * len(args),
        out_specs=[VMEM] * n,
        out_shape=[pltpu.VMEM(total.shape[1:], BF)] * n,
        compiler_params=pltpu.CompilerParams(vmem_limit_bytes=12 << 20),
        cost_estimate=pl.CostEstimate(flops=2 * total.size, bytes_accessed=10 * total.size, transcendentals=0),
        name="add",
    )(*args)


def fsum(parts):
    total = parts[0].astype(F32)
    for p in parts[1:]:
        total = total + p.astype(F32)
    return total


def body(tokens, expert_ids, route_share, gate_weight, up_weight, down_weight):
    expert = lax.axis_index("expert")
    place = lax.axis_index("blk")
    where = jnp.reshape(place, (1,))
    tokens, where = lax.optimization_barrier((tokens, where))
    c = place % 2
    gate_w, up_w, down_w = gate_weight[0], up_weight[0], down_weight[0]
    half = tokens.shape[2]
    rows = tokens.shape[1]

    mine = jnp.where(c == 0, tokens[0], tokens[1])
    theirs = jnp.where(c == 0, tokens[1], tokens[0])
    got = move_core(theirs)
    pair = jnp.where(
        c == 0, jnp.concatenate([mine, got], axis=1), jnp.concatenate([got, mine], axis=1)
    )
    two = SIDE // 2
    ids = jnp.where(c == 0, expert_ids[1], expert_ids[0])
    share = jnp.where(c == 0, route_share[1], route_share[0])
    names = (expert + jnp.arange(SIDE, dtype=jnp.int32)) % SIDE
    factors = jnp.where(ids[:, 0] == names[:, None], share, 0.0) + jnp.where(ids[:, 1] == names[:, None], 1.0 - share, 0.0)
    gate_w, up_w, t0 = load_call([gate_w, up_w], [pair, factors])
    (owners,) = gather_call(
        [pair] + [move_expert(pair, d) for d in FAR_FIRST],
        [(1, SIDE * rows, 2 * half)],
        [[(0, (0, slice(d * rows, (d + 1) * rows)), ...)] for d in (0, *FAR_FIRST)],
        [t0],
    )
    down_w, t1 = load_call([down_w], [owners])
    (line,) = gather_call(
        [owners] + [move_small(owners, d) for d in FAR_FIRST],
        [(SIDE, SIDE * rows, 2 * half)],
        [[(0, slice(d, d + 1), ...)] for d in (0, *FAR_FIRST)],
        [t1],
    )

    def at(sign, other, d, blocks=range(SIDE)):
        return [(sign, other, d, k) for k in blocks]


    def up(pieces, blocks, carry, final=False, behind=()):
        *sums, token = up_call(pieces, where, blocks, gate_w, up_w, carry, final, behind)
        return sums, token

    def down(h, blocks, adds, splits, dtype=BF, behind=()):
        return down_call(h, where, blocks, down_w, adds, splits, dtype, behind)

    right, left = move_bulk(line, 1), move_bulk(line, 3)
    other_line = move_core(line)
    own_sum, t0 = up([line], at(-1, 0, 0), None)
    other_sum, t1 = up([other_line], at(-1, 1, 0), None, False, [t0])
    right, left = after(right, t1), after(left, t1)
    shape = (two,) + line.shape[1:]
    (send_a,) = gather_call([right], [shape], [[(0, slice(None), slice(two))]], [t1])
    (send_b,) = gather_call([left], [shape], [[(0, slice(None), slice(two, SIDE))]], [t1])
    far_a, far_b = move_bulk(send_a, 1), move_bulk(send_b, 3)
    other_near = [move_core(after(right, send_a, send_b)), move_core(after(left, send_a, send_b))]
    own_sum, t0 = up([right, left], at(-1, 0, 1) + at(-1, 0, 3), own_sum, False, [send_a, send_b])
    other_sum, t1 = up(other_near, at(-1, 1, 1) + at(-1, 1, 3), other_sum, False, [t0])
    far_a, far_b = after(far_a, t1), after(far_b, t1)
    other_far = [move_core(far_a), move_core(far_b)]
    (h_own,), t0 = up([far_a, far_b], at(-1, 0, 2), own_sum, True)

    (send2,) = down(h_own, at(1, 1, 2), [], [SIDE])
    sent2 = move_core(send2)
    (h_other,), t1 = up(other_far, at(-1, 1, 2), other_sum, True, [send2])
    (send1,) = down(h_own, at(1, 1, 1), [], [SIDE], BF, [t1])
    (send3,) = down(h_own, at(1, 1, 3), [], [SIDE], BF, [t1])
    sent1, sent3 = move_core(send1), move_core(send3)
    m2a, m2b = down(h_other, at(1, 0, 2), [(sent2, 0)], [two, two], BF, [send1, send3])
    step_a, step_b = move_bulk(m2a, 1), move_bulk(m2b, 3)
    sent0 = move_core(down(h_own, at(1, 1, 0), [], [SIDE], BF, [m2a])[0])
    others = range(1, SIDE)
    (m1,) = down(h_other, at(1, 0, 1, others), [(sent1, 1), (step_a, 1)], [SIDE - 1])
    (m3,) = down(h_other, at(1, 0, 3, others), [(sent3, 1), (step_b, 1 - two)], [SIDE - 1])
    n1, n3 = move_bulk(m1, 1), move_bulk(m3, 3)
    (m1_own,) = down(h_other, at(1, 0, 1, [0]), [(sent1, 0), (step_a, 0)], [1], BF, [m1, m3])
    (m3_own,) = down(h_other, at(1, 0, 3, [0]), [(sent3, 0)], [1], BF, [m1, m3])
    m0_own, m0 = down(h_other, at(1, 0, 0), [(sent0, 0)], [1, SIDE - 1], F32, [m1, m3])
    s1, s2, s3 = add_call(m0, n1, n3)
    moved = [move_small(s2, 2), move_small(s1, 1), move_small(s3, 3)]
    own1, own3 = gather_call([m1_own, m3_own], [m1_own.shape] * 2, [[(0, ..., ...)], [(1, ..., ...)]], [s1])
    n1_own, n3_own = move_bulk(own1, 1), move_bulk(own3, 3)
    plane = fsum([m0_own[0], n1_own[0], n3_own[0]] + moved).astype(BF)
    plane = plane.reshape(SIDE, rows, 2 * half)

    total = 0.0
    for d in (0, *FAR_FIRST):
        back = plane[d] if d == 0 else move_expert(plane[d], -d)
        total = total + factors[d][:, None] * back.astype(F32)
    total = total.astype(BF)
    low, high = total[:, :half], total[:, half:]
    keep = jnp.where(c == 0, low, high)
    came = move_core(jnp.where(c == 0, high, low))
    return jnp.stack([jnp.where(c == 0, came, keep), jnp.where(c == 0, keep, came)])


def solution(mesh):
    return jax.shard_map(
        body,
        mesh=mesh,
        in_specs=(
            P(None, "expert", "blk"),
            P(None, "expert", None),
            P(None, "expert"),
            P("expert", None, "blk"),
            P("expert", None, "blk"),
            P("expert", "blk", None),
        ),
        out_specs=P(None, "expert", "blk"),
        check_vma=False,
    )
```

```python
import jax
import jax.numpy as jnp
from jax import lax
from jax.experimental import pallas as pl
from jax.experimental.pallas import tpu as pltpu
from jax.sharding import PartitionSpec as P

SIDE = 4
FAR_FIRST = (2, 1, 3)
BF = jnp.bfloat16
F32 = jnp.float32


def blk_perm(bulk, shift):
    pairs = []
    for z in range(SIDE):
        for x in range(SIDE):
            for c in range(2):
                along_z = (c == 0) == bulk
                z2 = (z + shift) % SIDE if along_z else z
                x2 = x if along_z else (x + shift) % SIDE
                pairs.append(((z * SIDE + x) * 2 + c, (z2 * SIDE + x2) * 2 + c))
    return pairs


def move_bulk(v, shift):
    return lax.ppermute(v, "blk", blk_perm(True, shift))


def move_small(v, shift):
    return lax.ppermute(v, "blk", blk_perm(False, shift))


def move_core(v):
    return lax.ppermute(v, "blk", [(i, i ^ 1) for i in range(2 * SIDE * SIDE)])


def move_expert(v, shift):
    return lax.ppermute(v, "expert", [(i, (i + shift) % SIDE) for i in range(SIDE)])


def feature_block(place, sign, other, bulk_shift, small_shift):
    z, x, core = place >> 3, (place >> 1) & (SIDE - 1), (place & 1) ^ other
    along_z = jnp.where(core == 0, sign * bulk_shift, sign * small_shift)
    along_x = jnp.where(core == 0, sign * small_shift, sign * bulk_shift)
    return ((z + along_z) & (SIDE - 1)) * SIDE + ((x + along_x) & (SIDE - 1))


def after(value, *others):
    return lax.optimization_barrier((value, *others))[0]


VMEM = pl.BlockSpec(memory_space=pltpu.VMEM)
SMEM = pl.BlockSpec(memory_space=pltpu.SMEM)
ANY = pl.BlockSpec(memory_space=pl.ANY)


def in_vmem(values):
    return [pltpu.with_memory_space_constraint(v, pltpu.VMEM) for v in values]


def up_call(pieces, place, blocks, gate_w, up_w, carry, final, behind):
    n = len(pieces)
    counts = [p.shape[0] for p in pieces]
    total = sum(counts)
    rows, width = pieces[0].shape[1:]
    cols = gate_w.shape[1]
    tile = 256

    def kernel(place_ref, *refs):
        xs = refs[:n]
        gate_ref, up_ref = refs[n : n + 2]
        rest = refs[n + 2 :]
        carried = rest[:2] if carry is not None else None
        outs = rest[(2 if carry is not None else 0) + len(behind) :]
        outs[-1][...] = jnp.zeros((8, 128), F32)
        x = jnp.concatenate([r[k] for r, m in zip(xs, counts) for k in range(m)], axis=1)
        at = [pl.multiple_of(feature_block(place_ref[0], *b) * width, width) for b in blocks]
        for j in range(cols // tile):
            cs = slice(j * tile, (j + 1) * tile)
            g = jnp.dot(x, jnp.concatenate([gate_ref[pl.ds(s, width), cs] for s in at], axis=0), preferred_element_type=F32)
            u = jnp.dot(x, jnp.concatenate([up_ref[pl.ds(s, width), cs] for s in at], axis=0), preferred_element_type=F32)
            if carried is not None:
                g = g + carried[0][:, cs]
                u = u + carried[1][:, cs]
            if final:
                outs[0][:, cs] = (g / (1.0 + jnp.exp(-g)) * u).astype(BF)
            else:
                outs[0][:, cs] = g
                outs[1][:, cs] = u

    args = in_vmem([*pieces, gate_w, up_w, *(carry or [])])
    if final:
        out_shape = [pltpu.VMEM((rows, cols), BF)]
    else:
        out_shape = [pltpu.VMEM((rows, cols), F32)] * 2
    out_shape.append(pltpu.VMEM((8, 128), F32))
    return pl.pallas_call(
        kernel,
        in_specs=[SMEM] + [VMEM] * len(args) + [ANY] * len(behind),
        out_specs=[VMEM] * len(out_shape),
        out_shape=out_shape,
        compiler_params=pltpu.CompilerParams(vmem_limit_bytes=12 << 20),
        cost_estimate=pl.CostEstimate(
            flops=2 * rows * total * width * cols * 2,
            bytes_accessed=total * width * cols * 4 + total * rows * width * 2 + rows * cols * 8,
            transcendentals=0,
        ),
        name="up",
    )(place, *args, *behind)


def down_call(hidden, place, blocks, down_w, adds, splits, dtype, behind):
    rows, depth = hidden.shape
    width = down_w.shape[1] // (SIDE * SIDE)
    n_add = len(adds)
    total = len(blocks)

    def kernel(place_ref, h_ref, w_ref, *rest):
        outs = [(o, k) for o, n in zip(rest[n_add + len(behind) :], splits) for k in range(n)]
        h = h_ref[...]
        for j in range(0, total, 2):
            at = [pl.multiple_of(feature_block(place_ref[0], *b) * width, width) for b in blocks[j : j + 2]]
            w = jnp.concatenate([w_ref[:, pl.ds(s, width)] for s in at], axis=1)
            y = jnp.dot(h, w, preferred_element_type=F32)
            for k in range(len(at)):
                part = y[:, k * width : (k + 1) * width]
                for ref, (v, first) in zip(rest, adds):
                    if 0 <= j + k + first < v.shape[0]:
                        part = part + ref[j + k + first].astype(F32)
                out, place = outs[j + k]
                out[place] = part.astype(dtype)

    args = in_vmem([hidden, down_w, *[v for v, _ in adds]])
    out_shape = [pltpu.VMEM((n, rows, width), dtype) for n in splits]
    return pl.pallas_call(
        kernel,
        in_specs=[SMEM] + [VMEM] * len(args) + [ANY] * len(behind),
        out_specs=[VMEM] * len(out_shape),
        out_shape=out_shape,
        compiler_params=pltpu.CompilerParams(vmem_limit_bytes=12 << 20),
        cost_estimate=pl.CostEstimate(
            flops=2 * rows * depth * width * total,
            bytes_accessed=total * width * (depth + rows * 2) * 2 + rows * depth * 2,
            transcendentals=0,
        ),
        name="down",
    )(place, *args, *behind)


def load_call(weights, behind):
    n = len(weights)

    def kernel(*refs):
        sem = refs[-1]
        refs[-2][...] = jnp.zeros((8, 128), F32)
        copies = [pltpu.make_async_copy(refs[k], refs[n + len(behind) + k], sem.at[k]) for k in range(n)]
        for copy in copies:
            copy.start()
        for copy in copies:
            copy.wait()

    return pl.pallas_call(
        kernel,
        in_specs=[pl.BlockSpec(memory_space=pltpu.HBM)] * n + [ANY] * len(behind),
        out_specs=[VMEM] * (n + 1),
        out_shape=[pltpu.VMEM(w.shape, w.dtype) for w in weights] + [pltpu.VMEM((8, 128), F32)],
        scratch_shapes=[pltpu.SemaphoreType.DMA((n,))],
        compiler_params=pltpu.CompilerParams(vmem_limit_bytes=1 << 20),
        cost_estimate=pl.CostEstimate(
            flops=0, bytes_accessed=4 * sum(w.size for w in weights), transcendentals=0
        ),
        name="load",
    )(*[pltpu.with_memory_space_constraint(w, pltpu.HBM) for w in weights], *behind)


def gather_call(pieces, out_shapes, places, behind):
    n = len(pieces)

    def kernel(*refs):
        for ref, to in zip(refs[:n], places):
            for k, index, part in to:
                refs[n + len(behind) + k][index] = ref[part]

    return pl.pallas_call(
        kernel,
        in_specs=[VMEM] * n + [ANY] * len(behind),
        out_specs=[VMEM] * len(out_shapes),
        out_shape=[pltpu.VMEM(shape, BF) for shape in out_shapes],
        compiler_params=pltpu.CompilerParams(vmem_limit_bytes=8 << 20),
        cost_estimate=pl.CostEstimate(
            flops=0, bytes_accessed=4 * sum(p.size for p in pieces), transcendentals=0
        ),
        name="gather",
    )(*in_vmem(pieces), *behind)


def add_call(total, *arrived):
    n = total.shape[0]

    def kernel(total_ref, *refs):
        for k in range(n):
            out = total_ref[k]
            for ref in refs[: len(arrived)]:
                out = out + ref[k].astype(F32)
            refs[len(arrived) + k][...] = out.astype(BF)

    args = in_vmem([total, *arrived])
    return pl.pallas_call(
        kernel,
        in_specs=[VMEM] * len(args),
        out_specs=[VMEM] * n,
        out_shape=[pltpu.VMEM(total.shape[1:], BF)] * n,
        compiler_params=pltpu.CompilerParams(vmem_limit_bytes=12 << 20),
        cost_estimate=pl.CostEstimate(flops=2 * total.size, bytes_accessed=10 * total.size, transcendentals=0),
        name="add",
    )(*args)


def fsum(parts):
    total = parts[0].astype(F32)
    for p in parts[1:]:
        total = total + p.astype(F32)
    return total


def body(tokens, expert_ids, route_share, gate_weight, up_weight, down_weight):
    expert = lax.axis_index("expert")
    place = lax.axis_index("blk")
    where = jnp.reshape(place, (1,))
    tokens, where = lax.optimization_barrier((tokens, where))
    c = place % 2
    gate_w, up_w, down_w = gate_weight[0], up_weight[0], down_weight[0]
    half = tokens.shape[2]
    rows = tokens.shape[1]

    mine = jnp.where(c == 0, tokens[0], tokens[1])
    theirs = jnp.where(c == 0, tokens[1], tokens[0])
    got = move_core(theirs)
    pair = jnp.where(
        c == 0, jnp.concatenate([mine, got], axis=1), jnp.concatenate([got, mine], axis=1)
    )
    two = SIDE // 2
    ids = jnp.where(c == 0, expert_ids[1], expert_ids[0])
    share = jnp.where(c == 0, route_share[1], route_share[0])
    names = (expert + jnp.arange(SIDE, dtype=jnp.int32)) % SIDE
    factors = jnp.where(ids[:, 0] == names[:, None], share, 0.0) + jnp.where(ids[:, 1] == names[:, None], 1.0 - share, 0.0)
    gate_w, up_w, t0 = load_call([gate_w, up_w], [pair, factors])
    (owners,) = gather_call(
        [pair] + [move_expert(pair, d) for d in FAR_FIRST],
        [(1, SIDE * rows, 2 * half)],
        [[(0, (0, slice(d * rows, (d + 1) * rows)), ...)] for d in (0, *FAR_FIRST)],
        [t0],
    )
    down_w, t1 = load_call([down_w], [owners])
    (line,) = gather_call(
        [owners] + [move_small(owners, d) for d in FAR_FIRST],
        [(SIDE, SIDE * rows, 2 * half)],
        [[(0, slice(d, d + 1), ...)] for d in (0, *FAR_FIRST)],
        [t1],
    )

    def at(sign, other, d, blocks=range(SIDE)):
        return [(sign, other, d, k) for k in blocks]


    def up(pieces, blocks, carry, final=False, behind=()):
        *sums, token = up_call(pieces, where, blocks, gate_w, up_w, carry, final, behind)
        return sums, token

    def down(h, blocks, adds, splits, dtype=BF, behind=()):
        return down_call(h, where, blocks, down_w, adds, splits, dtype, behind)

    right, left = move_bulk(line, 1), move_bulk(line, 3)
    other_line = move_core(line)
    own_sum, t0 = up([line], at(-1, 0, 0), None)
    other_sum, t1 = up([other_line], at(-1, 1, 0), None, False, [t0])
    right, left = after(right, t1), after(left, t1)
    shape = (two,) + line.shape[1:]
    send_a, send_b = gather_call(
        [right, left],
        [shape] * 2,
        [[(0, slice(None), slice(two))], [(1, slice(None), slice(two, SIDE))]],
        [t1],
    )
    far_a, far_b = move_bulk(send_a, 1), move_bulk(send_b, 3)
    other_near = [move_core(after(right, send_a, send_b)), move_core(after(left, send_a, send_b))]
    own_sum, t0 = up([right, left], at(-1, 0, 1) + at(-1, 0, 3), own_sum, False, [send_a, send_b])
    other_sum, t1 = up(other_near, at(-1, 1, 1) + at(-1, 1, 3), other_sum, False, [t0])
    far_a, far_b = after(far_a, t1), after(far_b, t1)
    other_far = [move_core(far_a), move_core(far_b)]
    (h_own,), t0 = up([far_a, far_b], at(-1, 0, 2), own_sum, True)

    (send2,) = down(h_own, at(1, 1, 2), [], [SIDE])
    sent2 = move_core(send2)
    (h_other,), t1 = up(other_far, at(-1, 1, 2), other_sum, True, [send2])
    (send1,) = down(h_own, at(1, 1, 1), [], [SIDE], BF, [t1])
    (send3,) = down(h_own, at(1, 1, 3), [], [SIDE], BF, [t1])
    (send0,) = down(h_own, at(1, 1, 0), [], [SIDE], BF, [send1, send3])
    sent1, sent3 = move_core(send1), move_core(send3)
    m2a, m2b = down(h_other, at(1, 0, 2), [(sent2, 0)], [two, two], BF, [send1, send3])
    step_a, step_b = move_bulk(m2a, 1), move_bulk(m2b, 3)
    sent0 = move_core(after(send0, m2a))
    others = range(1, SIDE)
    (m1,) = down(h_other, at(1, 0, 1, others), [(sent1, 1), (step_a, 1)], [SIDE - 1])
    (m3,) = down(h_other, at(1, 0, 3, others), [(sent3, 1), (step_b, 1 - two)], [SIDE - 1])
    n1, n3 = move_bulk(m1, 1), move_bulk(m3, 3)
    (m1_own,) = down(h_other, at(1, 0, 1, [0]), [(sent1, 0), (step_a, 0)], [1], BF, [m1, m3])
    (m3_own,) = down(h_other, at(1, 0, 3, [0]), [(sent3, 0)], [1], BF, [m1, m3])
    m0_own, m0 = down(h_other, at(1, 0, 0), [(sent0, 0)], [1, SIDE - 1], F32, [m1, m3])
    s1, s2, s3 = add_call(m0, n1, n3)
    moved = [move_small(s2, 2), move_small(s1, 1), move_small(s3, 3)]
    n1_own, n3_own = move_bulk(after(m1_own, n1), 1), move_bulk(after(m3_own, n3), 3)
    plane = fsum([m0_own[0], n1_own[0], n3_own[0]] + moved).astype(BF)
    plane = plane.reshape(SIDE, rows, 2 * half)

    total = 0.0
    for d in (0, *FAR_FIRST):
        back = plane[d] if d == 0 else move_expert(plane[d], -d)
        total = total + factors[d][:, None] * back.astype(F32)
    total = total.astype(BF)
    low, high = total[:, :half], total[:, half:]
    keep = jnp.where(c == 0, low, high)
    came = move_core(jnp.where(c == 0, high, low))
    return jnp.stack([jnp.where(c == 0, came, keep), jnp.where(c == 0, keep, came)])


def solution(mesh):
    return jax.shard_map(
        body,
        mesh=mesh,
        in_specs=(
            P(None, "expert", "blk"),
            P(None, "expert", None),
            P(None, "expert"),
            P("expert", None, "blk"),
            P("expert", None, "blk"),
            P("expert", "blk", None),
        ),
        out_specs=P(None, "expert", "blk"),
        check_vma=False,
    )
```

```python
import jax
import jax.numpy as jnp
from jax import lax
from jax.experimental import pallas as pl
from jax.experimental.pallas import tpu as pltpu
from jax.sharding import PartitionSpec as P

SIDE = 4
FAR_FIRST = (2, 1, 3)
BF = jnp.bfloat16
F32 = jnp.float32


def blk_perm(bulk, shift):
    pairs = []
    for z in range(SIDE):
        for x in range(SIDE):
            for c in range(2):
                along_z = (c == 0) == bulk
                z2 = (z + shift) % SIDE if along_z else z
                x2 = x if along_z else (x + shift) % SIDE
                pairs.append(((z * SIDE + x) * 2 + c, (z2 * SIDE + x2) * 2 + c))
    return pairs


def move_bulk(v, shift):
    return lax.ppermute(v, "blk", blk_perm(True, shift))


def move_small(v, shift):
    return lax.ppermute(v, "blk", blk_perm(False, shift))


def move_core(v):
    return lax.ppermute(v, "blk", [(i, i ^ 1) for i in range(2 * SIDE * SIDE)])


def move_expert(v, shift):
    return lax.ppermute(v, "expert", [(i, (i + shift) % SIDE) for i in range(SIDE)])


def feature_block(place, sign, other, bulk_shift, small_shift):
    z, x, core = place >> 3, (place >> 1) & (SIDE - 1), (place & 1) ^ other
    along_z = jnp.where(core == 0, sign * bulk_shift, sign * small_shift)
    along_x = jnp.where(core == 0, sign * small_shift, sign * bulk_shift)
    return ((z + along_z) & (SIDE - 1)) * SIDE + ((x + along_x) & (SIDE - 1))


def after(value, *others):
    return lax.optimization_barrier((value, *others))[0]


VMEM = pl.BlockSpec(memory_space=pltpu.VMEM)
SMEM = pl.BlockSpec(memory_space=pltpu.SMEM)
ANY = pl.BlockSpec(memory_space=pl.ANY)


def in_vmem(values):
    return [pltpu.with_memory_space_constraint(v, pltpu.VMEM) for v in values]


def up_call(pieces, place, blocks, gate_w, up_w, carry, final, behind):
    n = len(pieces)
    counts = [p.shape[0] for p in pieces]
    total = sum(counts)
    rows, width = pieces[0].shape[1:]
    cols = gate_w.shape[1]
    tile = 256

    def kernel(place_ref, *refs):
        xs = refs[:n]
        gate_ref, up_ref = refs[n : n + 2]
        rest = refs[n + 2 :]
        carried = rest[:2] if carry is not None else None
        outs = rest[(2 if carry is not None else 0) + len(behind) :]
        outs[-1][...] = jnp.zeros((8, 128), F32)
        x = jnp.concatenate([r[k] for r, m in zip(xs, counts) for k in range(m)], axis=1)
        at = [pl.multiple_of(feature_block(place_ref[0], *b) * width, width) for b in blocks]
        for j in range(cols // tile):
            cs = slice(j * tile, (j + 1) * tile)
            g = jnp.dot(x, jnp.concatenate([gate_ref[pl.ds(s, width), cs] for s in at], axis=0), preferred_element_type=F32)
            u = jnp.dot(x, jnp.concatenate([up_ref[pl.ds(s, width), cs] for s in at], axis=0), preferred_element_type=F32)
            if carried is not None:
                g = g + carried[0][:, cs]
                u = u + carried[1][:, cs]
            if final:
                outs[0][:, cs] = (g / (1.0 + jnp.exp(-g)) * u).astype(BF)
            else:
                outs[0][:, cs] = g
                outs[1][:, cs] = u

    args = in_vmem([*pieces, gate_w, up_w, *(carry or [])])
    if final:
        out_shape = [pltpu.VMEM((rows, cols), BF)]
    else:
        out_shape = [pltpu.VMEM((rows, cols), F32)] * 2
    out_shape.append(pltpu.VMEM((8, 128), F32))
    return pl.pallas_call(
        kernel,
        in_specs=[SMEM] + [VMEM] * len(args) + [ANY] * len(behind),
        out_specs=[VMEM] * len(out_shape),
        out_shape=out_shape,
        compiler_params=pltpu.CompilerParams(vmem_limit_bytes=12 << 20),
        cost_estimate=pl.CostEstimate(
            flops=2 * rows * total * width * cols * 2,
            bytes_accessed=total * width * cols * 4 + total * rows * width * 2 + rows * cols * 8,
            transcendentals=0,
        ),
        name="up",
    )(place, *args, *behind)


def down_call(hidden, place, blocks, down_w, adds, splits, dtype, behind):
    rows, depth = hidden.shape
    width = down_w.shape[1] // (SIDE * SIDE)
    n_add = len(adds)
    total = len(blocks)

    def kernel(place_ref, h_ref, w_ref, *rest):
        outs = [(o, k) for o, n in zip(rest[n_add + len(behind) :], splits) for k in range(n)]
        h = h_ref[...]
        for j in range(0, total, 2):
            at = [pl.multiple_of(feature_block(place_ref[0], *b) * width, width) for b in blocks[j : j + 2]]
            w = jnp.concatenate([w_ref[:, pl.ds(s, width)] for s in at], axis=1)
            y = jnp.dot(h, w, preferred_element_type=F32)
            for k in range(len(at)):
                part = y[:, k * width : (k + 1) * width]
                for ref, (v, first) in zip(rest, adds):
                    if 0 <= j + k + first < v.shape[0]:
                        part = part + ref[j + k + first].astype(F32)
                out, place = outs[j + k]
                out[place] = part.astype(dtype)

    args = in_vmem([hidden, down_w, *[v for v, _ in adds]])
    out_shape = [pltpu.VMEM((n, rows, width), dtype) for n in splits]
    return pl.pallas_call(
        kernel,
        in_specs=[SMEM] + [VMEM] * len(args) + [ANY] * len(behind),
        out_specs=[VMEM] * len(out_shape),
        out_shape=out_shape,
        compiler_params=pltpu.CompilerParams(vmem_limit_bytes=12 << 20),
        cost_estimate=pl.CostEstimate(
            flops=2 * rows * depth * width * total,
            bytes_accessed=total * width * (depth + rows * 2) * 2 + rows * depth * 2,
            transcendentals=0,
        ),
        name="down",
    )(place, *args, *behind)


def load_call(weights, behind):
    n = len(weights)

    def kernel(*refs):
        sem = refs[-1]
        refs[-2][...] = jnp.zeros((8, 128), F32)
        copies = [pltpu.make_async_copy(refs[k], refs[n + len(behind) + k], sem.at[k]) for k in range(n)]
        for copy in copies:
            copy.start()
        for copy in copies:
            copy.wait()

    return pl.pallas_call(
        kernel,
        in_specs=[pl.BlockSpec(memory_space=pltpu.HBM)] * n + [ANY] * len(behind),
        out_specs=[VMEM] * (n + 1),
        out_shape=[pltpu.VMEM(w.shape, w.dtype) for w in weights] + [pltpu.VMEM((8, 128), F32)],
        scratch_shapes=[pltpu.SemaphoreType.DMA((n,))],
        compiler_params=pltpu.CompilerParams(vmem_limit_bytes=1 << 20),
        cost_estimate=pl.CostEstimate(
            flops=0, bytes_accessed=4 * sum(w.size for w in weights), transcendentals=0
        ),
        name="load",
    )(*[pltpu.with_memory_space_constraint(w, pltpu.HBM) for w in weights], *behind)


def gather_call(pieces, out_shapes, places, behind):
    n = len(pieces)

    def kernel(*refs):
        for ref, to in zip(refs[:n], places):
            for k, index, part in to:
                refs[n + len(behind) + k][index] = ref[part]

    return pl.pallas_call(
        kernel,
        in_specs=[VMEM] * n + [ANY] * len(behind),
        out_specs=[VMEM] * len(out_shapes),
        out_shape=[pltpu.VMEM(shape, BF) for shape in out_shapes],
        compiler_params=pltpu.CompilerParams(vmem_limit_bytes=8 << 20),
        cost_estimate=pl.CostEstimate(
            flops=0, bytes_accessed=4 * sum(p.size for p in pieces), transcendentals=0
        ),
        name="gather",
    )(*in_vmem(pieces), *behind)


def add_call(total, *arrived):
    n = total.shape[0]

    def kernel(total_ref, *refs):
        for k in range(n):
            out = total_ref[k]
            for ref in refs[: len(arrived)]:
                out = out + ref[k].astype(F32)
            refs[len(arrived) + k][...] = out.astype(BF)

    args = in_vmem([total, *arrived])
    return pl.pallas_call(
        kernel,
        in_specs=[VMEM] * len(args),
        out_specs=[VMEM] * n,
        out_shape=[pltpu.VMEM(total.shape[1:], BF)] * n,
        compiler_params=pltpu.CompilerParams(vmem_limit_bytes=12 << 20),
        cost_estimate=pl.CostEstimate(flops=2 * total.size, bytes_accessed=10 * total.size, transcendentals=0),
        name="add",
    )(*args)


def fsum(parts):
    total = parts[0].astype(F32)
    for p in parts[1:]:
        total = total + p.astype(F32)
    return total


def body(tokens, expert_ids, route_share, gate_weight, up_weight, down_weight):
    expert = lax.axis_index("expert")
    place = lax.axis_index("blk")
    where = jnp.reshape(place, (1,))
    tokens, where = lax.optimization_barrier((tokens, where))
    c = place % 2
    gate_w, up_w, down_w = gate_weight[0], up_weight[0], down_weight[0]
    half = tokens.shape[2]
    rows = tokens.shape[1]

    mine = jnp.where(c == 0, tokens[0], tokens[1])
    theirs = jnp.where(c == 0, tokens[1], tokens[0])
    got = move_core(theirs)
    pair = jnp.where(
        c == 0, jnp.concatenate([mine, got], axis=1), jnp.concatenate([got, mine], axis=1)
    )
    two = SIDE // 2
    ids = jnp.where(c == 0, expert_ids[1], expert_ids[0])
    share = jnp.where(c == 0, route_share[1], route_share[0])
    names = (expert + jnp.arange(SIDE, dtype=jnp.int32)) % SIDE
    factors = jnp.where(ids[:, 0] == names[:, None], share, 0.0) + jnp.where(ids[:, 1] == names[:, None], 1.0 - share, 0.0)
    gate_w, up_w, t0 = load_call([gate_w, up_w], [pair, factors])
    (owners,) = gather_call(
        [pair] + [move_expert(pair, d) for d in FAR_FIRST],
        [(1, SIDE * rows, 2 * half)],
        [[(0, (0, slice(d * rows, (d + 1) * rows)), ...)] for d in (0, *FAR_FIRST)],
        [t0],
    )
    down_w, t1 = load_call([down_w], [owners])
    (line,) = gather_call(
        [owners] + [move_small(owners, d) for d in FAR_FIRST],
        [(SIDE, SIDE * rows, 2 * half)],
        [[(0, slice(d, d + 1), ...)] for d in (0, *FAR_FIRST)],
        [t1],
    )

    def at(sign, other, d, blocks=range(SIDE)):
        return [(sign, other, d, k) for k in blocks]


    def up(pieces, blocks, carry, final=False, behind=()):
        *sums, token = up_call(pieces, where, blocks, gate_w, up_w, carry, final, behind)
        return sums, token

    def down(h, blocks, adds, splits, dtype=BF, behind=()):
        return down_call(h, where, blocks, down_w, adds, splits, dtype, behind)

    right, left = move_bulk(line, 1), move_bulk(line, 3)
    other_line = move_core(line)
    own_sum, t0 = up([line], at(-1, 0, 0), None)
    other_sum, t1 = up([other_line], at(-1, 1, 0), None, False, [t0])
    right, left = after(right, t1), after(left, t1)
    shape = (two,) + line.shape[1:]
    send_a, send_b = gather_call(
        [right, left],
        [shape] * 2,
        [[(0, slice(None), slice(two))], [(1, slice(None), slice(two, SIDE))]],
        [t1],
    )
    far_a, far_b = move_bulk(send_a, 1), move_bulk(send_b, 3)
    other_near = [move_core(after(right, send_a, send_b)), move_core(after(left, send_a, send_b))]
    own_sum, t0 = up([right, left], at(-1, 0, 1) + at(-1, 0, 3), own_sum, False, [send_a, send_b])
    other_sum, t1 = up(other_near, at(-1, 1, 1) + at(-1, 1, 3), other_sum, False, [t0])
    far_a, far_b = after(far_a, t1), after(far_b, t1)
    other_far = [move_core(far_a), move_core(far_b)]
    (h_own,), t0 = up([far_a, far_b], at(-1, 0, 2), own_sum, True)

    (send2,) = down(h_own, at(1, 1, 2), [], [SIDE])
    sent2 = move_core(send2)
    (h_other,), t1 = up(other_far, at(-1, 1, 2), other_sum, True, [send2])
    (send1,) = down(h_own, at(1, 1, 1), [], [SIDE], BF, [t1])
    (send3,) = down(h_own, at(1, 1, 3), [], [SIDE], BF, [t1])
    (send0,) = down(h_own, at(1, 1, 0), [], [SIDE], BF, [send1, send3])
    sent1, sent3 = move_core(send1), move_core(send3)
    m2a, m2b = down(h_other, at(1, 0, 2), [(sent2, 0)], [two, two], BF, [send1, send3])
    step_a, step_b = move_bulk(m2a, 1), move_bulk(m2b, 3)
    sent0 = move_core(after(send0, m2a))
    others = range(1, SIDE)
    (m1,) = down(h_other, at(1, 0, 1, others), [(sent1, 1), (step_a, 1)], [SIDE - 1])
    (m3,) = down(h_other, at(1, 0, 3, others), [(sent3, 1), (step_b, 1 - two)], [SIDE - 1])
    n1, n3 = move_bulk(m1, 1), move_bulk(m3, 3)
    (m1_own,) = down(h_other, at(1, 0, 1, [0]), [(sent1, 0), (step_a, 0)], [1], BF, [m1, m3])
    (m3_own,) = down(h_other, at(1, 0, 3, [0]), [(sent3, 0)], [1], BF, [m1, m3])
    m0_own, m0 = down(h_other, at(1, 0, 0), [(sent0, 0)], [1, SIDE - 1], F32, [m1, m3])
    s1, s2, s3 = add_call(m0, n1, n3)
    moved = [move_small(s2, 2), move_small(s1, 1), move_small(s3, 3)]
    n1_own, n3_own = move_bulk(after(m1_own, n1), 1), move_bulk(after(m3_own, n1), 3)
    plane = fsum([m0_own[0], n1_own[0], n3_own[0]] + moved).astype(BF)
    plane = plane.reshape(SIDE, rows, 2 * half)

    total = 0.0
    for d in (0, *FAR_FIRST):
        back = plane[d] if d == 0 else move_expert(plane[d], -d)
        total = total + factors[d][:, None] * back.astype(F32)
    total = total.astype(BF)
    low, high = total[:, :half], total[:, half:]
    keep = jnp.where(c == 0, low, high)
    came = move_core(jnp.where(c == 0, high, low))
    return jnp.stack([jnp.where(c == 0, came, keep), jnp.where(c == 0, keep, came)])


def solution(mesh):
    return jax.shard_map(
        body,
        mesh=mesh,
        in_specs=(
            P(None, "expert", "blk"),
            P(None, "expert", None),
            P(None, "expert"),
            P("expert", None, "blk"),
            P("expert", None, "blk"),
            P("expert", "blk", None),
        ),
        out_specs=P(None, "expert", "blk"),
        check_vma=False,
    )
```
